32 devices in a mesh: phase: 4 (over y, x), slab: 8 (over z, core).
Axes of the slice: x: 2, y: 2, z: 4, core: 2. Of those that a mesh axis runs over, the one named last changes fastest.
Arguments:
- images: float32 [8, 256, 64, 128], P('phase', 'slab'), may hold values from -8 to 8, as said below
Outputs:
- forces: float32 [3, 8, 256, 64, 128], P(None, 'phase', 'slab')
The draws below stay inside these ranges and needn't reach their ends.
Inputs may be any that keep to these rules, and one draw needn't show every extreme that they name: `images`: Breathing-phase volumes of one body.
All inputs are finite; a program needn't handle non-finite values.
Results may differ from the reference program's by a relative error of at most 0.0001.
Values sent between devices are 32-bit elements; how exact they have to be, the bound alone decides.
No kernel may reach another device: no remote copies, remote signals or barrier semaphores. Data moves between devices by JAX's collectives and lax.ppermute only.
A program may use at most 128 MiB of HBM per device.

```python
import jax
import jax.numpy as jnp
from jax import lax

CY = 64
CX = 128
PHASES = 8
NZ = 256


def draw_images(key, part):
    shape = (PHASES, NZ, CY, CX)
    anatomy_key = jax.random.fold_in(key, 11)
    noise_key = jax.random.fold_in(key, 23)
    scale_key = jax.random.fold_in(key, 37)
    anatomy = jax.random.normal(anatomy_key, (NZ, CY, CX), jnp.float32)
    noise = 0.6 * jax.random.normal(noise_key, shape, jnp.float32)
    scales = jax.random.uniform(scale_key, (PHASES,), jnp.float32, 0.8, 1.2)
    images = scales[:, None, None, None] * anatomy[None] + noise
    return jnp.clip(images, -8.0, 8.0)


def setup_inputs(seed: int = 0) -> dict:
    keys = jax.random.split(jax.random.key(seed), 2)
    return {
        "images": draw_images(jax.random.fold_in(keys[1], 71), 0),
    }


EPSILON = 1e-5


def window_mean(field):
    summed = field
    for direction in range(3):
        widths = [(4, 4) if dimension == direction else (0, 0) for dimension in range(3)]
        padded = jnp.pad(summed, widths)
        length = summed.shape[direction]
        summed = sum(lax.slice_in_dim(padded, offset, offset + length, axis=direction) for offset in range(9))
    return summed / 729.0


def pair_terms(left_field, right_field):
    mean_left = window_mean(left_field)
    mean_right = window_mean(right_field)
    spread_left = window_mean(left_field * left_field) - mean_left * mean_left
    spread_right = window_mean(right_field * right_field) - mean_right * mean_right
    covariance = window_mean(left_field * right_field) - mean_left * mean_right
    offset_left = left_field - mean_left
    offset_right = right_field - mean_right
    weight = 2.0 * covariance / (spread_left * spread_right + EPSILON)
    toward_left = weight * (offset_right - covariance / (spread_left + EPSILON) * offset_left)
    toward_right = weight * (offset_left - covariance / (spread_right + EPSILON) * offset_right)
    return toward_left, toward_right


def gradient(field):
    padded = jnp.pad(field, 1)
    along_z = (padded[2:, 1:-1, 1:-1] - padded[:-2, 1:-1, 1:-1]) * 0.5
    along_y = (padded[1:-1, 2:, 1:-1] - padded[1:-1, :-2, 1:-1]) * 0.5
    along_x = (padded[1:-1, 1:-1, 2:] - padded[1:-1, 1:-1, :-2]) * 0.5
    return jnp.stack([along_z, along_y, along_x])


def reference(images):
    coefs = jnp.zeros_like(images)
    for distance in (1, 2):
        partner = jnp.roll(images, -distance, axis=0)
        toward_own, toward_partner = lax.map(lambda couple: pair_terms(couple[0], couple[1]), (images, partner))
        coefs = coefs + toward_own + jnp.roll(toward_partner, distance, axis=0)
    forces = lax.map(lambda couple: gradient(couple[0]) * couple[1][None], (images, coefs))
    return jnp.transpose(forces, (1, 0, 2, 3, 4))
```

```python
import functools

import jax
import jax.numpy as jnp
from jax import lax
from jax.experimental import pallas as pl
from jax.experimental.pallas import tpu as pltpu
from jax.sharding import PartitionSpec as P

EPSILON = 1e-05
CELLS = 729.0
BLOCK = 4
VMEM = pl.BlockSpec(memory_space=pltpu.VMEM)
SMEM = pl.BlockSpec(memory_space=pltpu.SMEM)
ANY = pl.BlockSpec(memory_space=pl.ANY)
GRANT = 16 << 20


def box_matrix(width):
    i = lax.broadcasted_iota(jnp.int32, (width, width), 0)
    j = lax.broadcasted_iota(jnp.int32, (width, width), 1)
    band = jnp.where(jnp.abs(i - j) <= 4, 1.0, 0.0).astype(jnp.bfloat16)
    return jnp.concatenate([band, band, band], axis=0)


def thirds(v):
    high = v.astype(jnp.bfloat16)
    rest = v - high.astype(jnp.float32)
    middle = rest.astype(jnp.bfloat16)
    low = (rest - middle.astype(jnp.float32)).astype(jnp.bfloat16)
    return jnp.concatenate([high, middle, low], axis=1)


def depth_sums(p):
    core = ((p[3] + p[4]) + (p[5] + p[6])) + (p[7] + p[8])
    a = p[1] + p[2]
    b = p[9] + p[10]
    return (core + (p[0] + a), core + (a + p[9]), core + (p[2] + b), core + (b + p[11]))


def clear_rims(tz, rows):
    zero = jnp.zeros((8, tz.shape[-1]), jnp.float32)
    for w in range(tz.shape[0]):
        for i in range(BLOCK):
            tz[w, i, 0:8, :] = zero
            tz[w, i, rows + 8 : rows + 16, :] = zero


def plane_sums(i, tz, t3, sx, box):
    windows, rows = tz.shape[0], tz.shape[2] - 16
    parts = []
    for w in range(windows):
        for k in range(rows // 8 + 1):
            r = 8 * k
            t3[i, w, r : r + 8, :] = (
                tz[w, i, r + 3 : r + 11, :] + tz[w, i, r + 4 : r + 12, :] + tz[w, i, r + 5 : r + 13, :]
            )
        parts.append(
            thirds(t3[i, w, 1 : rows + 1, :] + t3[i, w, 4 : rows + 4, :] + t3[i, w, 7 : rows + 7, :])
        )
    sums = jnp.dot(jnp.concatenate(parts, axis=0), box, preferred_element_type=jnp.float32)
    for w in range(windows):
        sx[w, i] = sums[rows * w : rows * (w + 1)]


def pair_weight(s_both, s_a, s_b, v_a, v_b):
    c = CELLS * s_both - s_a * s_b
    return c, c * (2.0 * CELLS * CELLS) / (v_a * v_b + EPSILON * CELLS**4)


def own_kernel(images, before, after, stats, acc, field, tz, t3, sx):
    depth, rows, width = images.shape[1:]
    clear_rims(tz, rows)
    for a in range(2):
        field[a, 0:BLOCK] = before[a]
        field[a, depth + BLOCK :] = after[a]

    @pl.loop(0, depth)
    def _(z):
        for a in range(2):
            field[a, z + BLOCK] = images[a, z]

    box = box_matrix(width)

    @pl.loop(0, depth // BLOCK)
    def _(j):
        base = j * BLOCK

        @pl.loop(0, rows // 8)
        def _(y):
            here = pl.ds(pl.multiple_of(y * 8, 8), 8)
            there = pl.ds(pl.multiple_of(y * 8 + 8, 8), 8)

            def put(w, planes):
                for i, v in enumerate(depth_sums(planes)):
                    tz[w, i, there, :] = v

            zero = [field[0, base + p, here, :] for p in range(12)]
            put(0, zero)
            put(1, [v * v for v in zero])
            one = [field[1, base + p, here, :] for p in range(12)]
            put(2, one)
            put(3, [v * v for v in one])
            put(4, [v * field[0, base + p, here, :] for p, v in enumerate(one)])

        for i in range(BLOCK):
            plane_sums(i, tz, t3, sx, box)
            z = base + i
            for y in range(0, rows, 8):
                r = slice(y, y + 8)
                s_0, q_0, s_1, q_1, both = [sx[w, i, r, :] for w in range(5)]
                v_0 = CELLS * q_0 - s_0 * s_0
                v_1 = CELLS * q_1 - s_1 * s_1
                c, g = pair_weight(both, s_0, s_1, v_0, v_1)
                stats[0, 0, z, r, :] = s_0
                stats[0, 1, z, r, :] = v_0
                stats[1, 0, z, r, :] = s_1
                stats[1, 1, z, r, :] = v_1
                acc[0, 0, z, r, :] = g * (images[1, z, r, :] - s_1 * (1.0 / CELLS))
                acc[1, 0, z, r, :] = g * (images[0, z, r, :] - s_0 * (1.0 / CELLS))
                gc = g * c
                acc[0, 1, z, r, :] = gc
                acc[1, 1, z, r, :] = gc


def side_block(j, near, own_plane, partner, images, stats, acc, acc_base, tz, t3, sx, box, sink):
    rows = images.shape[2]
    far = 1 - near
    own_near, own_far = far, near

    @pl.loop(0, rows // 8)
    def _(y):
        here = pl.ds(pl.multiple_of(y * 8, 8), 8)
        there = pl.ds(pl.multiple_of(y * 8 + 8, 8), 8)

        def theirs(a, p):
            return partner[p // BLOCK][a, p % BLOCK, here, :]

        def put(w, planes):
            for i, v in enumerate(depth_sums(planes)):
                tz[w, i, there, :] = v

        n = [theirs(near, p) for p in range(12)]
        put(0, n)
        put(1, [v * v for v in n])
        put(2, [v * own_plane(own_near, p, here) for p, v in enumerate(n)])
        put(3, [v * own_plane(own_far, p, here) for p, v in enumerate(n)])
        f = [theirs(far, p) for p in range(12)]
        put(4, f)
        put(5, [v * v for v in f])
        put(6, [v * own_plane(own_near, p, here) for p, v in enumerate(f)])

    for i in range(BLOCK):
        plane_sums(i, tz, t3, sx, box)
        z = BLOCK * j + i
        for y in range(0, rows, 8):
            r = slice(y, y + 8)
            s_n, q_n, nn, fn, s_f, q_f, nf = [sx[w, i, r, :] for w in range(7)]
            o_s, o_v = stats[own_near, 0, z, r, :], stats[own_near, 1, z, r, :]
            p_s, p_v = stats[own_far, 0, z, r, :], stats[own_far, 1, z, r, :]
            v_n = CELLS * q_n - s_n * s_n
            v_f = CELLS * q_f - s_f * s_f
            off_n = partner[1][near, i, r, :] - s_n * (1.0 / CELLS)
            off_f = partner[1][far, i, r, :] - s_f * (1.0 / CELLS)
            c_nn, g_nn = pair_weight(nn, o_s, s_n, o_v, v_n)
            c_nf, g_nf = pair_weight(nf, o_s, s_f, o_v, v_f)
            c_fn, g_fn = pair_weight(fn, p_s, s_n, p_v, v_n)
            b = acc_base + i
            sink(own_near, i, r, acc[own_near, 0, b, r, :] + g_nn * off_n + g_nf * off_f,
                 acc[own_near, 1, b, r, :] + g_nn * c_nn + g_nf * c_nf, o_s, o_v)
            sink(own_far, i, r, acc[own_far, 0, b, r, :] + g_fn * off_n,
                 acc[own_far, 1, b, r, :] + g_fn * c_fn, p_s, p_v)


def own_planes(j, images, before, after):
    depth = images.shape[1]

    def plane(a, p, rows):
        z = BLOCK * (j - 1) + p
        if z < 0:
            return before[a, z + BLOCK, rows, :]
        if z >= depth:
            return after[a, z - depth, rows, :]
        return images[a, z, rows, :]

    return plane


def first_kernel(j, near_ref, p0, p1, p2, images, before, after, stats, acc, out, tz, t3, sx):
    near = near_ref[0]
    clear_rims(tz, images.shape[2])

    def sink(a, i, r, one, two, s, v):
        out[a, 0, i, r, :] = one
        out[a, 1, i, r, :] = two

    side_block(j, near, own_planes(j, images, before, after), (p0, p1, p2), images, stats, acc,
               BLOCK * j, tz, t3, sx, box_matrix(images.shape[3]), sink)


def last_kernel(js, chained, near_ref, *refs):
    partner = refs[: len(js) + 2]
    accs = refs[len(js) + 2 : 2 * len(js) + 2]
    rest = refs[2 * len(js) + 2 :]
    if chained:
        images, before, after, stats, _, out, tz, t3, sx, coef, padded, block, sems = rest
    else:
        images, before, after, stats, out, tz, t3, sx, coef, padded, block, sems = rest
    near = near_ref[0]
    depth, rows, width = images.shape[1:]
    clear_rims(tz, rows)
    zero = jnp.zeros((8, width), jnp.float32)
    for a in range(2):
        padded[a, 0:8, :] = zero
        padded[a, rows + 8 : rows + 16, :] = zero
    lane = lax.broadcasted_iota(jnp.int32, (8, width), 1)
    box = box_matrix(width)
    copies = []
    for n, j in enumerate(js):
        own = own_planes(j, images, before, after)

        def sink(a, i, r, one, two, s, v):
            here = images[a, BLOCK * j + i, r, :]
            coef[a, i, r, :] = 0.5 * (
                one - two / (v + EPSILON * CELLS * CELLS) * (here - s * (1.0 / CELLS))
            )

        side_block(j, near, own, partner[n : n + 3], images, stats, accs[n], 0, tz, t3, sx, box, sink)
        for i in range(BLOCK):
            for a in range(2):
                padded[a, 8 : rows + 8, :] = images[a, BLOCK * j + i]
                for y in range(0, rows, 8):
                    r = slice(y, y + 8)
                    c = coef[a, i, r, :]
                    block[n, 0, a, i, r, :] = c * (own(a, i + 5, r) - own(a, i + 3, r))
                    block[n, 1, a, i, r, :] = c * (padded[a, y + 9 : y + 17, :] - padded[a, y + 7 : y + 15, :])
                    v = padded[a, y + 8 : y + 16, :]
                    after_x = jnp.where(lane < width - 1, pltpu.roll(v, width - 1, 1), 0.0)
                    before_x = jnp.where(lane > 0, pltpu.roll(v, 1, 1), 0.0)
                    block[n, 2, a, i, r, :] = c * (after_x - before_x)
        copy = pltpu.make_async_copy(block.at[n], out.at[:, :, BLOCK * j : BLOCK * (j + 1)], sems.at[n])
        copy.start()
        copies.append(copy)
    for copy in copies:
        copy.wait()


def scratches(windows, rows, width):
    return [
        pltpu.VMEM((windows, BLOCK, rows + 16, width), jnp.float32),
        pltpu.VMEM((BLOCK, windows, rows + 8, width), jnp.float32),
        pltpu.VMEM((windows, BLOCK, rows, width), jnp.float32),
    ]


def params():
    return pltpu.CompilerParams(vmem_limit_bytes=GRANT)


def like(*shape):
    return jax.ShapeDtypeStruct(shape, jnp.float32)


def own_terms(images, before, after):
    _, depth, rows, width = images.shape
    return pl.pallas_call(
        own_kernel,
        out_shape=(like(2, 2, depth, rows, width), like(2, 2, depth, rows, width)),
        in_specs=[VMEM] * 3,
        out_specs=(VMEM, VMEM),
        scratch_shapes=[pltpu.VMEM((2, depth + 2 * BLOCK, rows, width), jnp.float32)] + scratches(5, rows, width),
        compiler_params=params(),
        name="own_terms",
    )(images, before, after)


def first_side(j, near, partner, images, before, after, stats, acc):
    rows, width = images.shape[2:]
    return pl.pallas_call(
        functools.partial(first_kernel, j),
        out_shape=like(2, 2, BLOCK, rows, width),
        in_specs=[SMEM] + [VMEM] * 8,
        out_specs=VMEM,
        scratch_shapes=scratches(7, rows, width),
        compiler_params=params(),
        name=f"first_side_{j}",
    )(near, *partner, images, before, after, stats, acc)


def last_side(js, near, partner, accs, images, before, after, stats, forces):
    _, depth, rows, width = images.shape
    chained = forces is not None
    operands = [near, *partner, *accs, images, before, after, stats] + ([forces] if chained else [])
    return pl.pallas_call(
        functools.partial(last_kernel, js, chained),
        out_shape=like(3, 2, depth, rows, width),
        in_specs=[SMEM] + [VMEM] * (2 * len(js) + 2 + 4) + ([ANY] if chained else []),
        out_specs=ANY,
        input_output_aliases={len(operands) - 1: 0} if chained else {},
        scratch_shapes=scratches(7, rows, width)
        + [
            pltpu.VMEM((2, BLOCK, rows, width), jnp.float32),
            pltpu.VMEM((2, rows + 16, width), jnp.float32),
            pltpu.VMEM((len(js), 3, 2, BLOCK, rows, width), jnp.float32),
            pltpu.SemaphoreType.DMA((len(js),)),
        ],
        compiler_params=params(),
        name=f"last_side_{js[0]}",
    )(*operands)


def across(value):
    n = lax.axis_size("phase")
    return lax.ppermute(value, "phase", [(q, q ^ 1) for q in range(n)])


def onward(value):
    n = lax.axis_size("phase")
    return lax.ppermute(value, "phase", [(q, (q + (2 if q % 2 == 0 else n - 2)) % n) for q in range(n)])


def upward(value):
    n = lax.axis_size("slab")
    return lax.ppermute(value, "slab", [(q, q + 1) for q in range(n - 1)])


def downward(value):
    n = lax.axis_size("slab")
    return lax.ppermute(value, "slab", [(q + 1, q) for q in range(n - 1)])


def local(images):
    count = images.shape[1] // BLOCK
    assert images.shape[0] == 2 and images.shape[1] % BLOCK == 0 and lax.axis_size("phase") % 2 == 0
    near = lax.rem(lax.axis_index("phase"), 2).astype(jnp.int32).reshape(1)
    blocks = [images[:, BLOCK * b : BLOCK * (b + 1)] for b in range(count)]
    order = [0, count - 1] + list(range(1, count - 1))

    one, two = [None] * count, [None] * count
    for b in order:
        one[b] = across(blocks[b])
    before, after = upward(blocks[-1]), downward(blocks[0])
    for b in order:
        two[b] = onward(one[b])
    low = upward(jnp.concatenate([one[-1], two[-1]], axis=0))
    high = downward(jnp.concatenate([one[0], two[0]], axis=0))
    one = [low[:2]] + one + [high[:2]]
    two = [low[2:]] + two + [high[2:]]

    stats, acc = own_terms(images, before, after)
    accs = [first_side(j, near, one[j : j + 3], images, before, after, stats, acc) for j in range(count)]
    forces = None
    groups = [(j,) for j in range(count - 3)] + [tuple(range(count - 3, count))]
    for js in groups:
        forces = last_side(js, 1 - near, two[js[0] : js[-1] + 3], [accs[j] for j in js], images, before, after, stats, forces)
    return forces


def solution(mesh):
    in_specs = (P("phase", "slab", None, None),)
    out_specs = P(None, "phase", "slab", None, None)
    return jax.shard_map(local, mesh=mesh, in_specs=in_specs, out_specs=out_specs, check_vma=False)
```

```python
import functools

import jax
import jax.numpy as jnp
from jax import lax
from jax.experimental import pallas as pl
from jax.experimental.pallas import tpu as pltpu
from jax.sharding import PartitionSpec as P


EPSILON = 1e-05
CELLS = 729.0
BLOCK = 4
VMEM = pl.BlockSpec(memory_space=pltpu.VMEM)
ANY = pl.BlockSpec(memory_space=pl.ANY)
GRANT = 10


def box_matrix(width):
    i = lax.broadcasted_iota(jnp.int32, (width, width), 0)
    j = lax.broadcasted_iota(jnp.int32, (width, width), 1)
    band = jnp.where(jnp.abs(i - j) <= 4, 1.0, 0.0).astype(jnp.bfloat16)
    return jnp.concatenate([band, band, band], axis=0)


def thirds(v):
    high = v.astype(jnp.bfloat16)
    rest = v - high.astype(jnp.float32)
    middle = rest.astype(jnp.bfloat16)
    low = (rest - middle.astype(jnp.float32)).astype(jnp.bfloat16)
    return jnp.concatenate([high, middle, low], axis=1)


def depth_sums(p):
    core = ((p[3] + p[4]) + (p[5] + p[6])) + (p[7] + p[8])
    a = p[1] + p[2]
    b = p[9] + p[10]
    return (core + (p[0] + a), core + (a + p[9]), core + (p[2] + b), core + (b + p[11]))


def clear_rims(tz, rows):
    zero = jnp.zeros((8, tz.shape[-1]), jnp.float32)
    for w in range(tz.shape[0]):
        for i in range(BLOCK):
            tz[w, i, 0:8, :] = zero
            tz[w, i, rows + 8 : rows + 16, :] = zero


def plane_sums(i, tz, t3, sx, box):
    windows, rows = tz.shape[0], tz.shape[2] - 16
    parts = []
    for w in range(windows):
        for k in range(rows // 8 + 1):
            r = 8 * k
            t3[i, w, r : r + 8, :] = (
                tz[w, i, r + 3 : r + 11, :] + tz[w, i, r + 4 : r + 12, :] + tz[w, i, r + 5 : r + 13, :]
            )
        parts.append(
            thirds(t3[i, w, 1 : rows + 1, :] + t3[i, w, 4 : rows + 4, :] + t3[i, w, 7 : rows + 7, :])
        )
    sums = jnp.dot(jnp.concatenate(parts, axis=0), box, preferred_element_type=jnp.float32)
    for w in range(windows):
        sx[w, i] = sums[rows * w : rows * (w + 1)]


def pair_weight(s_both, s_a, s_b, v_a, v_b):
    c = CELLS * s_both - s_a * s_b
    return c, c * (2.0 * CELLS * CELLS) / (v_a * v_b + EPSILON * CELLS**4)


def plane_of(parts, base):
    def read(a, p, rows):
        z = base + p
        for ref, offset, first, length in parts:
            if first <= z < first + length:
                return ref[a + offset, z - first, rows, :]
        raise ValueError("plane")

    return read


def own_block(read, stats, acc, z_out, tz, t3, sx, box):
    rows = tz.shape[2] - 16

    @pl.loop(0, rows // 8)
    def _(y):
        here = pl.ds(pl.multiple_of(y * 8, 8), 8)
        there = pl.ds(pl.multiple_of(y * 8 + 8, 8), 8)

        def put(w, planes):
            for i, v in enumerate(depth_sums(planes)):
                tz[w, i, there, :] = v

        zero = [read(0, p, here) for p in range(12)]
        put(0, zero)
        put(1, [v * v for v in zero])
        one = [read(1, p, here) for p in range(12)]
        put(2, one)
        put(3, [v * v for v in one])
        put(4, [v * read(0, p, here) for p, v in enumerate(one)])

    for i in range(BLOCK):
        plane_sums(i, tz, t3, sx, box)
        for y in range(0, rows, 8):
            r = slice(y, y + 8)
            s_0, q_0, s_1, q_1, both = [sx[w, i, r, :] for w in range(5)]
            v_0 = CELLS * q_0 - s_0 * s_0
            v_1 = CELLS * q_1 - s_1 * s_1
            c, g = pair_weight(both, s_0, s_1, v_0, v_1)
            z = z_out + i
            stats[0, 0, z, r, :] = s_0
            stats[0, 1, z, r, :] = v_0
            stats[1, 0, z, r, :] = s_1
            stats[1, 1, z, r, :] = v_1
            acc[0, 0, z, r, :] = g * (read(1, BLOCK + i, r) - s_1 * (1.0 / CELLS))
            acc[1, 0, z, r, :] = g * (read(0, BLOCK + i, r) - s_0 * (1.0 / CELLS))
            gc = g * c
            acc[0, 1, z, r, :] = gc
            acc[1, 1, z, r, :] = gc


def own_inner_kernel(size, *refs):
    parts, (stats, acc, field, tz, t3, sx) = refs[: size + 2], refs[size + 2 :]
    rows, width = parts[0].shape[2:]
    clear_rims(tz, rows)
    box = box_matrix(width)
    for k, part in enumerate(parts):
        for a in range(2):
            field[a, BLOCK * k : BLOCK * (k + 1)] = part[a]

    @pl.loop(0, size)
    def _(j):
        own_block(lambda a, p, rows: field[a, BLOCK * j + p, rows, :], stats, acc, BLOCK * j, tz, t3, sx, box)


def own_ends_kernel(low, high, first, second, third, fourth, stats, acc, field, tz, t3, sx):
    rows, width = first.shape[2:]
    clear_rims(tz, rows)
    box = box_matrix(width)
    for e, parts in enumerate(((low, first, second), (third, fourth, high))):
        for k, part in enumerate(parts):
            for a in range(2):
                field[e, a, BLOCK * k : BLOCK * (k + 1)] = part[a]

    @pl.loop(0, 2)
    def _(e):
        own_block(lambda a, p, rows: field[e, a, p, rows, :], stats, acc, BLOCK * e, tz, t3, sx, box)


def side_block(near, own, theirs, centre, stats, stats_base, acc, acc_base, tz, t3, sx, box, sink):
    rows = tz.shape[2] - 16
    far = 1 - near
    own_near, own_far = far, near

    @pl.loop(0, rows // 8)
    def _(y):
        here = pl.ds(pl.multiple_of(y * 8, 8), 8)
        there = pl.ds(pl.multiple_of(y * 8 + 8, 8), 8)

        def put(w, planes):
            for i, v in enumerate(depth_sums(planes)):
                tz[w, i, there, :] = v

        n = [theirs(near, p, here) for p in range(12)]
        put(0, n)
        put(1, [v * v for v in n])
        put(2, [v * own(own_near, p, here) for p, v in enumerate(n)])
        put(3, [v * own(own_far, p, here) for p, v in enumerate(n)])
        f = [theirs(far, p, here) for p in range(12)]
        put(4, f)
        put(5, [v * v for v in f])
        put(6, [v * own(own_near, p, here) for p, v in enumerate(f)])

    for i in range(BLOCK):
        plane_sums(i, tz, t3, sx, box)
        z = stats_base + i
        b = acc_base + i
        for y in range(0, rows, 8):
            r = slice(y, y + 8)
            s_n, q_n, nn, fn, s_f, q_f, nf = [sx[w, i, r, :] for w in range(7)]
            o_s, o_v = stats[own_near, 0, z, r, :], stats[own_near, 1, z, r, :]
            p_s, p_v = stats[own_far, 0, z, r, :], stats[own_far, 1, z, r, :]
            v_n = CELLS * q_n - s_n * s_n
            v_f = CELLS * q_f - s_f * s_f
            off_n = centre[near, i, r, :] - s_n * (1.0 / CELLS)
            off_f = centre[far, i, r, :] - s_f * (1.0 / CELLS)
            c_nn, g_nn = pair_weight(nn, o_s, s_n, o_v, v_n)
            c_nf, g_nf = pair_weight(nf, o_s, s_f, o_v, v_f)
            c_fn, g_fn = pair_weight(fn, p_s, s_n, p_v, v_n)
            sink(own_near, i, r, acc[own_near, 0, b, r, :] + g_nn * off_n + g_nf * off_f,
                 acc[own_near, 1, b, r, :] + g_nn * c_nn + g_nf * c_nf, o_s, o_v)
            sink(own_far, i, r, acc[own_far, 0, b, r, :] + g_fn * off_n,
                 acc[own_far, 1, b, r, :] + g_fn * c_fn, p_s, p_v)


def readers(j, count, side, refs):
    depth = BLOCK * count
    own = [(ref, 0, BLOCK * k[1], BLOCK) for k, ref in refs.items() if k[0] == "own"]
    theirs = [(ref, 0, BLOCK * k[1], BLOCK) for k, ref in refs.items() if k[0] == "side"]
    for name, first in (("low", -BLOCK), ("high", depth)):
        if (name,) in refs:
            own.append((refs[name,], 0, first, BLOCK))
            theirs.append((refs[name,], 2 * side, first, BLOCK))
    base = BLOCK * (j - 1)
    return plane_of(own, base), plane_of(theirs, base)


def split_refs(keys, refs):
    return dict(zip(keys, refs[: len(keys)])), refs[len(keys) :]


def first_kernel(j, count, stats_base, keys, *refs):
    refs, (out, tz, t3, sx) = split_refs(keys, refs)
    near = lax.rem(lax.axis_index("phase"), 2)
    rows, width = refs["own", j].shape[2:]
    clear_rims(tz, rows)
    own, theirs = readers(j, count, 1, refs)

    def sink(a, i, r, one, two, s, v):
        out[a, 0, i, r, :] = one
        out[a, 1, i, r, :] = two

    side_block(near, own, theirs, refs["side", j], refs["stats", j], stats_base, refs["acc", j], stats_base,
               tz, t3, sx, box_matrix(width), sink)


def last_kernel(js, count, bases, keys, *refs):
    refs, (out, tz, t3, sx, coef, padded, block, sems) = split_refs(keys, refs)
    near = 1 - lax.rem(lax.axis_index("phase"), 2)
    rows, width = refs["own", js[0]].shape[2:]
    clear_rims(tz, rows)
    zero = jnp.zeros((8, width), jnp.float32)
    for a in range(2):
        padded[a, 0:8, :] = zero
        padded[a, rows + 8 : rows + 16, :] = zero
    lane = lax.broadcasted_iota(jnp.int32, (8, width), 1)
    box = box_matrix(width)
    copies = []
    for n, j in enumerate(js):
        own, theirs = readers(j, count, 2, refs)

        def sink(a, i, r, one, two, s, v):
            here = own(a, BLOCK + i, r)
            coef[a, i, r, :] = 0.5 * (
                one - two / (v + EPSILON * CELLS * CELLS) * (here - s * (1.0 / CELLS))
            )

        side_block(near, own, theirs, refs["side", j], refs["stats", j], bases[n], refs["acc", j], 0,
                   tz, t3, sx, box, sink)
        for i in range(BLOCK):
            for a in range(2):
                padded[a, 8 : rows + 8, :] = refs["own", j][a, i]
                for y in range(0, rows, 8):
                    r = slice(y, y + 8)
                    c = coef[a, i, r, :]
                    block[n, 0, a, i, r, :] = c * (own(a, i + 5, r) - own(a, i + 3, r))
                    block[n, 1, a, i, r, :] = c * (padded[a, y + 9 : y + 17, :] - padded[a, y + 7 : y + 15, :])
                    v = padded[a, y + 8 : y + 16, :]
                    after_x = jnp.where(lane < width - 1, pltpu.roll(v, width - 1, 1), 0.0)
                    before_x = jnp.where(lane > 0, pltpu.roll(v, 1, 1), 0.0)
                    block[n, 2, a, i, r, :] = c * (after_x - before_x)
        copy = pltpu.make_async_copy(block.at[n], out.at[:, :, BLOCK * j : BLOCK * (j + 1)], sems.at[n])
        copy.start()
        copies.append(copy)
    for copy in copies:
        copy.wait()


def scratches(windows, rows, width):
    return [
        pltpu.VMEM((windows, BLOCK, rows + 16, width), jnp.float32),
        pltpu.VMEM((BLOCK, windows, rows + 8, width), jnp.float32),
        pltpu.VMEM((windows, BLOCK, rows, width), jnp.float32),
    ]


def params(mib=GRANT):
    return pltpu.CompilerParams(vmem_limit_bytes=mib << 20)


def like(*shape):
    return jax.ShapeDtypeStruct(shape, jnp.float32)


def cut_kernel(bs, images, *refs):
    outs, sems = refs[:-1], refs[-1]
    copies = [
        pltpu.make_async_copy(images.at[:, BLOCK * b : BLOCK * (b + 1)], outs[n], sems.at[n]) for n, b in enumerate(bs)
    ]
    for copy in copies:
        copy.start()
    for copy in copies:
        copy.wait()


def cut_blocks(bs, images, mib):
    phases, _, rows, width = images.shape
    outs = pl.pallas_call(
        functools.partial(cut_kernel, bs),
        out_shape=[like(phases, BLOCK, rows, width)] * len(bs),
        in_specs=[pl.BlockSpec(memory_space=pltpu.HBM)],
        out_specs=[VMEM] * len(bs),
        scratch_shapes=[pltpu.SemaphoreType.DMA((len(bs),))],
        compiler_params=params(mib),
    )(pltpu.with_memory_space_constraint(images, pltpu.HBM))
    return dict(zip(bs, outs))


def pack_kernel(*refs):
    for n in range(2):
        for k in range(3):
            for a in range(2):
                refs[6 + n][2 * k + a] = refs[3 * n + k][a]


def packed(groups):
    shape = groups[0][0].shape
    out = like(3 * shape[0], *shape[1:])
    return pl.pallas_call(
        pack_kernel,
        out_shape=(out, out),
        in_specs=[VMEM] * 6,
        out_specs=(VMEM, VMEM),
        compiler_params=params(6),
        name="pack",
    )(*groups[0], *groups[1])


def own_inner(low, high, blocks):
    rows, width = blocks[low].shape[2:]
    size = high - low
    shape = like(2, 2, BLOCK * size, rows, width)
    return pl.pallas_call(
        functools.partial(own_inner_kernel, size),
        out_shape=(shape, shape),
        in_specs=[VMEM] * (size + 2),
        out_specs=(VMEM, VMEM),
        scratch_shapes=[pltpu.VMEM((2, BLOCK * (size + 2), rows, width), jnp.float32)] + scratches(5, rows, width),
        compiler_params=params(),
    )(*[blocks[b] for b in range(low - 1, high + 1)])


def own_ends(low, high, *blocks):
    rows, width = low.shape[2:]
    shape = like(2, 2, 2 * BLOCK, rows, width)
    return pl.pallas_call(
        own_ends_kernel,
        out_shape=(shape, shape),
        in_specs=[VMEM] * 6,
        out_specs=(VMEM, VMEM),
        scratch_shapes=[pltpu.VMEM((2, 2, 3 * BLOCK, rows, width), jnp.float32)] + scratches(5, rows, width),
        compiler_params=params(),
        name="own_ends",
    )(low, high, *blocks)


def gather_operands(js, count, own, side, low, high):
    wanted = {}
    for j in js:
        for b in (j - 1, j, j + 1):
            if b < 0:
                wanted["low",] = low
            elif b >= count:
                wanted["high",] = high
            else:
                wanted["own", b] = own[b]
                wanted["side", b] = side[b]
    return wanted


def specs_of(wanted):
    return [ANY if k == ("forces",) else VMEM for k in wanted]


def first_side(j, count, own, side, low, high, stats, acc, base):
    rows, width = low.shape[2:]
    wanted = gather_operands((j,), count, own, side, low, high)
    wanted["stats", j], wanted["acc", j] = stats, acc
    return pl.pallas_call(
        functools.partial(first_kernel, j, count, base, tuple(wanted)),
        out_shape=like(2, 2, BLOCK, rows, width),
        in_specs=specs_of(wanted),
        out_specs=VMEM,
        scratch_shapes=scratches(7, rows, width),
        compiler_params=params(),
    )(*wanted.values())


def last_side(js, count, own, side, low, high, stats, bases, accs, forces):
    rows, width = low.shape[2:]
    depth = BLOCK * count
    wanted = gather_operands(js, count, own, side, low, high)
    for j in js:
        wanted["stats", j] = stats[j]
        wanted["acc", j] = accs[j]
    if forces is not None:
        wanted["forces",] = forces
    return pl.pallas_call(
        functools.partial(last_kernel, js, count, [bases[j] for j in js], tuple(wanted)),
        out_shape=like(3, 2, depth, rows, width),
        in_specs=specs_of(wanted),
        out_specs=ANY,
        input_output_aliases={len(wanted) - 1: 0} if forces is not None else {},
        scratch_shapes=scratches(7, rows, width)
        + [
            pltpu.VMEM((2, BLOCK, rows, width), jnp.float32),
            pltpu.VMEM((2, rows + 16, width), jnp.float32),
            pltpu.VMEM((len(js), 3, 2, BLOCK, rows, width), jnp.float32),
            pltpu.SemaphoreType.DMA((len(js),)),
        ],
        compiler_params=params(),
    )(*wanted.values())


def across(value):
    n = lax.axis_size("phase")
    return lax.ppermute(value, "phase", [(q, q ^ 1) for q in range(n)])


def onward(value):
    n = lax.axis_size("phase")
    return lax.ppermute(value, "phase", [(q, (q + (2 if q % 2 == 0 else n - 2)) % n) for q in range(n)])


def upward(value):
    n = lax.axis_size("slab")
    return lax.ppermute(value, "slab", [(q, q + 1) for q in range(n - 1)])


def downward(value):
    n = lax.axis_size("slab")
    return lax.ppermute(value, "slab", [(q + 1, q) for q in range(n - 1)])


def local_forces(images):
    count = images.shape[1] // BLOCK
    assert images.shape[0] == 2 and images.shape[1] == BLOCK * count and count >= 6
    assert lax.axis_size("phase") % 2 == 0
    half = (count + 1) // 2

    blocks = cut_blocks((0, count - 1), images, 4)
    blocks.update(cut_blocks(tuple(range(1, count - 1)), images, 4))
    one = {b: across(blocks[b]) for b in blocks}
    two = {b: onward(one[b]) for b in blocks}
    top, end = 0, count - 1
    low, high = packed([(blocks[end], one[end], two[end]), (blocks[top], one[top], two[top])])
    low, high = upward(low), downward(high)

    near_half = own_inner(1, half, blocks)
    far_half = own_inner(half, count - 1, blocks)
    outer = own_ends(low, high, blocks[0], blocks[1], blocks[end - 1], blocks[end])
    stats, acc, base = {}, {}, {}
    for j in range(count):
        if j in (0, count - 1):
            (stats[j], acc[j]), base[j] = outer, 0 if j == 0 else BLOCK
        elif j < half:
            (stats[j], acc[j]), base[j] = near_half, BLOCK * (j - 1)
        else:
            (stats[j], acc[j]), base[j] = far_half, BLOCK * (j - half)
    sums = {
        j: first_side(j, count, blocks, one, low, high, stats[j], acc[j], base[j]) for j in range(count)
    }
    forces = None
    for js in last_groups(count):
        forces = last_side(js, count, blocks, two, low, high, stats, base, sums, forces)
    return forces


def last_groups(count):
    return [(j,) for j in [1, 2, 0] + list(range(3, count - 3))] + [tuple(range(count - 3, count))]


def solution(mesh):
    in_specs = (P("phase", "slab", None, None),)
    out_specs = P(None, "phase", "slab", None, None)
    return jax.shard_map(local_forces, mesh=mesh, in_specs=in_specs, out_specs=out_specs, check_vma=False)
```

```python
import functools

import jax
import jax.numpy as jnp
from jax import lax
from jax.experimental import pallas as pl
from jax.experimental.pallas import tpu as pltpu
from jax.sharding import PartitionSpec as P


EPSILON = 1e-05
CELLS = 729.0
BLOCK = 4
GROUPS = {5: ((0, 1, 2), (3, 4)), 7: ((0, 1, 2), (3, 4), (5, 6))}
VMEM = pl.BlockSpec(memory_space=pltpu.VMEM)
ANY = pl.BlockSpec(memory_space=pl.ANY)
GRANT = 12


def box_matrix(width):
    i = lax.broadcasted_iota(jnp.int32, (width, width), 0)
    j = lax.broadcasted_iota(jnp.int32, (width, width), 1)
    return jnp.where(jnp.abs(i - j) <= 4, 1.0, 0.0).astype(jnp.bfloat16)


def thirds(v):
    high = v.astype(jnp.bfloat16)
    rest = v - high.astype(jnp.float32)
    middle = rest.astype(jnp.bfloat16)
    low = (rest - middle.astype(jnp.float32)).astype(jnp.bfloat16)
    return high, middle, low


def depth_sums(read, planes):
    sums = []
    while len(sums) < planes:
        base = len(sums)
        if planes - base >= 8:
            back = [read(base + 7)]
            for k in range(6, -1, -1):
                back.append(back[-1] + read(base + k))
            ahead = read(base + 8)
            sums.append(back[7] + ahead)
            for k in range(1, 8):
                ahead = ahead + read(base + 8 + k)
                sums.append(back[7 - k] + ahead)
        else:
            p = [read(base + k) for k in range(12)]
            core = ((p[3] + p[4]) + (p[5] + p[6])) + (p[7] + p[8])
            a = p[1] + p[2]
            b = p[9] + p[10]
            sums += [core + (p[0] + a), core + (a + p[9]), core + (p[2] + b), core + (b + p[11])]
    return sums


def clear_rims(tz, rows):
    zero = jnp.zeros((8, tz.shape[-1]), jnp.float32)
    for w in range(tz.shape[0]):
        for i in range(tz.shape[1]):
            tz[w, i, 0:8, :] = zero
            tz[w, i, rows + 8 : rows + 16, :] = zero


def plane_sums(i, tz, t3, sx, box):
    windows, rows = tz.shape[0], tz.shape[2] - 16
    e = i % BLOCK
    for w in range(windows):
        for r in range(0, rows + 8, 8):
            t3[e, w, r : r + 8, :] = (
                tz[w, i, r + 3 : r + 11, :] + tz[w, i, r + 4 : r + 12, :] + tz[w, i, r + 5 : r + 13, :]
            )
    for group in GROUPS[windows]:
        parts = [
            thirds(t3[e, w, 1 : rows + 1, :] + t3[e, w, 4 : rows + 4, :] + t3[e, w, 7 : rows + 7, :]) for w in group
        ]
        sums = None
        for t in range(3):
            term = jnp.dot(
                jnp.concatenate([p[t] for p in parts], axis=0), box, preferred_element_type=jnp.float32
            )
            sums = term if sums is None else sums + term
        for k, w in enumerate(group):
            sx[w, e] = sums[rows * k : rows * (k + 1)]


def pair_weight(s_both, s_a, m_b, v_a, v_b):
    c = s_both - s_a * m_b
    return c, c / (v_a * v_b + EPSILON * CELLS * CELLS)


def row_blocks(rows, body):
    @pl.loop(0, rows // 16)
    def _(y):
        for half in range(2):
            r = pl.multiple_of(y * 16 + 8 * half, 8)
            body(pl.ds(r, 8), pl.ds(pl.multiple_of(r + 8, 8), 8))


def plane_of(parts, base):
    def read(a, p, rows):
        z = base + p
        for ref, offset, first, length in parts:
            if first <= z < first + length:
                return ref[a + offset, z - first, rows, :]
        raise ValueError("plane")

    return read


def own_block(read, stats, acc, z_out, tz, t3, sx, box):
    rows = tz.shape[2] - 16

    def body(here, there):
        zero = [read(0, p, here) for p in range(3 * BLOCK)]
        one = [read(1, p, here) for p in range(3 * BLOCK)]
        terms = [
            lambda p: zero[p],
            lambda p: zero[p] * zero[p],
            lambda p: one[p],
            lambda p: one[p] * one[p],
            lambda p: zero[p] * one[p],
        ]
        for w, term in enumerate(terms):
            for i, v in enumerate(depth_sums(term, BLOCK)):
                tz[w, i, there, :] = v

    row_blocks(rows, body)

    for i in range(BLOCK):
        plane_sums(i, tz, t3, sx, box)
        for y in range(0, rows, 8):
            r = slice(y, y + 8)
            s_0, q_0, s_1, q_1, both = [sx[w, i, r, :] for w in range(5)]
            m_0, m_1 = s_0 * (1.0 / CELLS), s_1 * (1.0 / CELLS)
            v_0 = q_0 - s_0 * m_0
            v_1 = q_1 - s_1 * m_1
            c, g = pair_weight(both, s_0, m_1, v_0, v_1)
            z = z_out + i
            stats[0, 0, z, r, :] = s_0
            stats[0, 1, z, r, :] = v_0
            stats[1, 0, z, r, :] = s_1
            stats[1, 1, z, r, :] = v_1
            acc[0, 0, z, r, :] = g * (read(1, BLOCK + i, r) - m_1)
            acc[1, 0, z, r, :] = g * (read(0, BLOCK + i, r) - m_0)
            gc = g * c
            acc[0, 1, z, r, :] = gc
            acc[1, 1, z, r, :] = gc


def own_inner_kernel(size, *refs):
    parts, (stats, acc, field, tz, t3, sx) = refs[: size + 2], refs[size + 2 :]
    rows, width = parts[0].shape[2:]
    clear_rims(tz, rows)
    box = box_matrix(width)
    for k, part in enumerate(parts):
        for a in range(2):
            field[a, BLOCK * k : BLOCK * (k + 1)] = part[a]

    @pl.loop(0, size)
    def _(j):
        own_block(lambda a, p, rows: field[a, BLOCK * j + p, rows, :], stats, acc, BLOCK * j, tz, t3, sx, box)


def own_ends_kernel(low, high, first, second, third, fourth, stats, acc, field, tz, t3, sx):
    rows, width = first.shape[2:]
    clear_rims(tz, rows)
    box = box_matrix(width)
    for e, parts in enumerate(((low, first, second), (third, fourth, high))):
        for k, part in enumerate(parts):
            for a in range(2):
                field[e, a, BLOCK * k : BLOCK * (k + 1)] = part[a]

    @pl.loop(0, 2)
    def _(e):
        own_block(lambda a, p, rows: field[e, a, p, rows, :], stats, acc, BLOCK * e, tz, t3, sx, box)


def side_group(planes, near, own, theirs, tables, tz, t3, sx, box, sink, done):
    rows = tz.shape[2] - 16
    far = 1 - near
    own_near, own_far = far, near

    def body(here, there):
        def n(p):
            return theirs(near, p, here)

        def f(p):
            return theirs(far, p, here)

        def square(read):
            def term(p):
                v = read(p)
                return v * v

            return term

        terms = [
            n,
            square(n),
            lambda p: n(p) * own(own_near, p, here),
            lambda p: n(p) * own(own_far, p, here),
            f,
            square(f),
            lambda p: f(p) * own(own_near, p, here),
        ]
        for w, term in enumerate(terms):
            for i, v in enumerate(depth_sums(term, planes)):
                tz[w, i, there, :] = v

    row_blocks(rows, body)

    for i in range(planes):
        plane_sums(i, tz, t3, sx, box)
        stats, z, acc, b = tables(i)
        for y in range(0, rows, 8):
            r = slice(y, y + 8)
            s_n, q_n, nn, fn, s_f, q_f, nf = [sx[w, i % BLOCK, r, :] for w in range(7)]
            o_s, o_v = stats[own_near, 0, z, r, :], stats[own_near, 1, z, r, :]
            p_s, p_v = stats[own_far, 0, z, r, :], stats[own_far, 1, z, r, :]
            m_n, m_f = s_n * (1.0 / CELLS), s_f * (1.0 / CELLS)
            v_n = q_n - s_n * m_n
            v_f = q_f - s_f * m_f
            off_n = theirs(near, BLOCK + i, r) - m_n
            off_f = theirs(far, BLOCK + i, r) - m_f
            c_nn, g_nn = pair_weight(nn, o_s, m_n, o_v, v_n)
            c_nf, g_nf = pair_weight(nf, o_s, m_f, o_v, v_f)
            c_fn, g_fn = pair_weight(fn, p_s, m_n, p_v, v_n)
            sink(own_near, i, r, acc[own_near, 0, b, r, :] + g_nn * off_n + g_nf * off_f,
                 acc[own_near, 1, b, r, :] + g_nn * c_nn + g_nf * c_nf, o_s, o_v)
            sink(own_far, i, r, acc[own_far, 0, b, r, :] + g_fn * off_n,
                 acc[own_far, 1, b, r, :] + g_fn * c_fn, p_s, p_v)
        done(i)


def readers(j, count, rims, refs):
    depth = BLOCK * count
    own = [(ref, 0, BLOCK * k[1], BLOCK) for k, ref in refs.items() if k[0] == "own"]
    theirs = [(ref, 0, BLOCK * k[1], BLOCK) for k, ref in refs.items() if k[0] == "side"]
    for name, first in (("low", -BLOCK), ("high", depth)):
        if (name,) in refs:
            own.append((refs[name,], 0, first, BLOCK))
            theirs.append((refs[name + rims[0],], rims[1], first, BLOCK))
    base = BLOCK * (j - 1)
    return plane_of(own, base), plane_of(theirs, base)


def split_refs(keys, refs):
    return dict(zip(keys, refs[: len(keys)])), refs[len(keys) :]


def first_kernel(js, count, bases, keys, *refs):
    refs, (out, tz, t3, sx) = split_refs(keys, refs)
    near = lax.rem(lax.axis_index("phase"), 2)
    rows, width = refs["own", js[0]].shape[2:]
    clear_rims(tz, rows)
    own, theirs = readers(js[0], count, ("", 2), refs)

    def tables(i):
        j, z = js[i // BLOCK], bases[i // BLOCK] + i % BLOCK
        return refs["stats", j], z, refs["acc", j], z

    def sink(a, i, r, one, two, s, v):
        out[a, 0, i, r, :] = one
        out[a, 1, i, r, :] = two

    side_group(BLOCK * len(js), near, own, theirs, tables, tz, t3, sx, box_matrix(width), sink, lambda i: None)


def last_kernel(js, count, bases, sums_base, before, final, keys, *refs):
    refs, rest = split_refs(keys, refs)
    if before is not None:
        out, rest = rest[0], rest[1:]
    if not final:
        block, rest = rest[0], rest[1:]
    tz, t3, sx, coef, padded, *rest = rest
    if final:
        block, rest = rest[0], rest[1:]
    planes = BLOCK * len(js)
    first = BLOCK * js[0]
    copies = []

    def write(source, first, sem):
        copy = pltpu.make_async_copy(source, out.at[:, :, first : first + source.shape[2]], sem)
        copy.start()
        copies.append(copy)

    if before is not None:
        sems = rest[0]
        write(refs["block",], BLOCK * before, sems.at[0])
    near = 1 - lax.rem(lax.axis_index("phase"), 2)
    rows, width = refs["own", js[0]].shape[2:]
    clear_rims(tz, rows)
    zero = jnp.zeros((8, width), jnp.float32)
    for a in range(2):
        padded[a, 0:8, :] = zero
        padded[a, rows + 8 : rows + 16, :] = zero
    lane = lax.broadcasted_iota(jnp.int32, (8, width), 1)
    own, theirs = readers(js[0], count, ("_b", 0), refs)

    def tables(i):
        j = js[i // BLOCK]
        return refs["stats", j], bases[i // BLOCK] + i % BLOCK, refs["acc", j], sums_base[i // BLOCK] + i % BLOCK

    def sink(a, i, r, one, two, s, v):
        here = own(a, BLOCK + i, r) - s * (1.0 / CELLS)
        coef[a, i % BLOCK, r, :] = CELLS * (one - two / (v + EPSILON * CELLS) * here)

    def forces(i):
        for a in range(2):
            padded[a, 8 : rows + 8, :] = own(a, BLOCK + i, slice(0, rows))
            for y in range(0, rows, 8):
                r = slice(y, y + 8)
                c = coef[a, i % BLOCK, r, :]
                block[0, a, i, r, :] = c * (own(a, i + 5, r) - own(a, i + 3, r))
                block[1, a, i, r, :] = c * (padded[a, y + 9 : y + 17, :] - padded[a, y + 7 : y + 15, :])
                v = padded[a, y + 8 : y + 16, :]
                after_x = jnp.where(lane < width - 1, pltpu.roll(v, width - 1, 1), 0.0)
                before_x = jnp.where(lane > 0, pltpu.roll(v, 1, 1), 0.0)
                block[2, a, i, r, :] = c * (after_x - before_x)

    starts = [0] + [i for i in range(BLOCK, planes, BLOCK)] + [planes - 2, planes]

    def done(i):
        if i + 1 in starts:
            low = max(k for k in starts if k <= i)
            for k in range(low, i + 1):
                forces(k)
            if final:
                write(block.at[:, :, low : i + 1], first + low, sems.at[1 + starts.index(low)])

    side_group(planes, near, own, theirs, tables, tz, t3, sx, box_matrix(width), sink, done)
    for copy in copies:
        copy.wait()


def scratches(windows, rows, width, blocks=1):
    return [
        pltpu.VMEM((windows, BLOCK * blocks, rows + 16, width), jnp.float32),
        pltpu.VMEM((BLOCK, windows, rows + 8, width), jnp.float32),
        pltpu.VMEM((windows, BLOCK, rows, width), jnp.float32),
    ]


def params(mib=GRANT):
    return pltpu.CompilerParams(vmem_limit_bytes=mib << 20)


def like(*shape):
    return jax.ShapeDtypeStruct(shape, jnp.float32)


def cut_kernel(bs, images, *refs):
    outs, sems = refs[:-1], refs[-1]
    copies = [
        pltpu.make_async_copy(images.at[:, BLOCK * b : BLOCK * (b + 1)], outs[n], sems.at[n]) for n, b in enumerate(bs)
    ]
    for copy in copies:
        copy.start()
    for copy in copies:
        copy.wait()


def cut_blocks(bs, images, mib):
    phases, _, rows, width = images.shape
    outs = pl.pallas_call(
        functools.partial(cut_kernel, bs),
        out_shape=[like(phases, BLOCK, rows, width)] * len(bs),
        in_specs=[pl.BlockSpec(memory_space=pltpu.HBM)],
        out_specs=[VMEM] * len(bs),
        scratch_shapes=[pltpu.SemaphoreType.DMA((len(bs),))],
        compiler_params=params(mib),
    )(pltpu.with_memory_space_constraint(images, pltpu.HBM))
    return dict(zip(bs, outs))


def pack_kernel(*refs):
    for n in range(2):
        for k in range(2):
            for a in range(2):
                refs[4 + n][2 * k + a] = refs[2 * n + k][a]


def packed(groups):
    shape = groups[0][0].shape
    out = like(2 * shape[0], *shape[1:])
    return pl.pallas_call(
        pack_kernel,
        out_shape=(out, out),
        in_specs=[VMEM] * 4,
        out_specs=(VMEM, VMEM),
        compiler_params=params(6),
        name="pack",
    )(*groups[0], *groups[1])


def own_inner(low, high, blocks):
    rows, width = blocks[low].shape[2:]
    size = high - low
    shape = like(2, 2, BLOCK * size, rows, width)
    return pl.pallas_call(
        functools.partial(own_inner_kernel, size),
        out_shape=(shape, shape),
        in_specs=[VMEM] * (size + 2),
        out_specs=(VMEM, VMEM),
        scratch_shapes=[pltpu.VMEM((2, BLOCK * (size + 2), rows, width), jnp.float32)] + scratches(5, rows, width),
        compiler_params=params(),
    )(*[blocks[b] for b in range(low - 1, high + 1)])


def own_ends(low, high, *blocks):
    rows, width = low.shape[2:]
    shape = like(2, 2, 2 * BLOCK, rows, width)
    return pl.pallas_call(
        own_ends_kernel,
        out_shape=(shape, shape),
        in_specs=[VMEM] * 6,
        out_specs=(VMEM, VMEM),
        scratch_shapes=[pltpu.VMEM((2, 2, 3 * BLOCK, rows, width), jnp.float32)] + scratches(5, rows, width),
        compiler_params=params(),
        name="own_ends",
    )(low, high, *blocks)


def gather_operands(js, count, own, side, rims):
    wanted = {}
    for b in range(js[0] - 1, js[-1] + 2):
        if 0 <= b < count:
            wanted["own", b] = own[b]
            wanted["side", b] = side[b]
        else:
            for name in rims:
                if name.startswith("low" if b < 0 else "high"):
                    wanted[name,] = rims[name]
    return wanted


def specs_of(wanted):
    return [ANY if k == ("forces",) else VMEM for k in wanted]


def first_side(js, count, own, side, rims, stats, accs, bases):
    rows, width = own[0].shape[2:]
    wanted = gather_operands(js, count, own, side, rims)
    for j in js:
        wanted["stats", j], wanted["acc", j] = stats[j], accs[j]
    return pl.pallas_call(
        functools.partial(first_kernel, js, count, [bases[j] for j in js], tuple(wanted)),
        out_shape=like(2, 2, BLOCK * len(js), rows, width),
        in_specs=specs_of(wanted),
        out_specs=VMEM,
        scratch_shapes=scratches(7, rows, width, len(js)),
        compiler_params=params(),
    )(*wanted.values())


def last_side(js, count, own, side, rims, stats, bases, sums, before, block, forces, final):
    rows, width = own[0].shape[2:]
    wanted = gather_operands(js, count, own, side, rims)
    for j in js:
        wanted["stats", j], wanted["acc", j] = stats[j], sums[j][0]
    if before is not None:
        wanted["block",] = block
    if forces is not None:
        wanted["forces",] = forces
    whole = like(3, 2, BLOCK * count, rows, width)
    piece = (3, 2, BLOCK * len(js), rows, width)
    outs = ([(whole, ANY)] if before is not None else []) + ([] if final else [(like(*piece), VMEM)])
    got = pl.pallas_call(
        functools.partial(
            last_kernel, js, count, [bases[j] for j in js], [sums[j][1] for j in js], before, final, tuple(wanted)
        ),
        out_shape=[shape for shape, _ in outs],
        in_specs=specs_of(wanted),
        out_specs=[spec for _, spec in outs],
        input_output_aliases={len(wanted) - 1: 0} if forces is not None else {},
        scratch_shapes=scratches(7, rows, width, len(js))
        + [pltpu.VMEM((2, BLOCK, rows, width), jnp.float32), pltpu.VMEM((2, rows + 16, width), jnp.float32)]
        + ([pltpu.VMEM(piece, jnp.float32)] if final else [])
        + ([pltpu.SemaphoreType.DMA((2 + len(js) if final else 1,))] if before is not None else []),
        compiler_params=params(),
    )(*wanted.values())
    forces = got[0] if before is not None else None
    return forces, None if final else got[-1]


def across(value):
    n = lax.axis_size("phase")
    return lax.ppermute(value, "phase", [(q, q ^ 1) for q in range(n)])


def onward(value):
    n = lax.axis_size("phase")
    return lax.ppermute(value, "phase", [(q, (q + (2 if q % 2 == 0 else n - 2)) % n) for q in range(n)])


def yonder(value):
    n = lax.axis_size("phase")
    return lax.ppermute(value, "phase", [(q, (q + (n - 2 if q % 2 == 0 else 2)) % n) for q in range(n)])


def upward(value):
    n = lax.axis_size("slab")
    return lax.ppermute(value, "slab", [(q, q + 1) for q in range(n - 1)])


def downward(value):
    n = lax.axis_size("slab")
    return lax.ppermute(value, "slab", [(q + 1, q) for q in range(n - 1)])


def local_forces(images):
    count = images.shape[1] // BLOCK
    assert images.shape[0] == 2 and images.shape[1] == BLOCK * count and count >= 6
    assert lax.axis_size("phase") % 2 == 0
    half = (count + 1) // 2

    top, end, turned = 0, count - 1, count - 2
    blocks = cut_blocks((top,), images, 4)
    blocks.update(cut_blocks((end, turned), images, 4))
    blocks.update(cut_blocks(tuple(range(1, turned)), images, 4))
    one = {b: across(blocks[b]) for b in blocks}
    two = {b: onward(one[b]) for b in blocks if b != turned}
    two[turned] = across(yonder(blocks[turned]))
    low, high = packed([(blocks[end], one[end]), (blocks[top], one[top])])
    rims = {"low": upward(low), "high": downward(high), "low_b": upward(two[end]), "high_b": downward(two[top])}

    near_half = own_inner(1, half, blocks)
    far_half = own_inner(half, count - 1, blocks)
    outer = own_ends(rims["low"], rims["high"], blocks[0], blocks[1], blocks[end - 1], blocks[end])
    stats, acc, base = {}, {}, {}
    for j in range(count):
        if j in (0, count - 1):
            (stats[j], acc[j]), base[j] = outer, 0 if j == 0 else BLOCK
        elif j < half:
            (stats[j], acc[j]), base[j] = near_half, BLOCK * (j - 1)
        else:
            (stats[j], acc[j]), base[j] = far_half, BLOCK * (j - half)
    shared = {name: rims[name] for name in ("low", "high")}
    sums = {}
    for js in first_groups(count):
        total = first_side(js, count, blocks, one, shared, stats, acc, base)
        sums.update({j: (total, BLOCK * k) for k, j in enumerate(js)})
    forces, block, before = None, None, None
    groups = last_groups(count)
    for js in groups:
        forces, block = last_side(
            js, count, blocks, two, rims, stats, base, sums, before, block, forces, js == groups[-1]
        )
        before = js[0]
    return forces


def first_groups(count):
    return [(j,) for j in range(count - 3)] + [tuple(range(count - 3, count))]


def last_groups(count):
    return [(j,) for j in range(count - 3)] + [tuple(range(count - 3, count))]


def solution(mesh):
    in_specs = (P("phase", "slab", None, None),)
    out_specs = P(None, "phase", "slab", None, None)
    return jax.shard_map(local_forces, mesh=mesh, in_specs=in_specs, out_specs=out_specs, check_vma=False)
```

```python
import functools

import jax
import jax.numpy as jnp
from jax import lax
from jax.experimental import pallas as pl
from jax.experimental.pallas import tpu as pltpu
from jax.sharding import PartitionSpec as P


EPSILON = 1e-05
CELLS = 729.0
BLOCK = 4
GROUPS = {5: ((0, 1, 2), (3, 4)), 7: ((0, 1, 2), (3, 4), (5, 6))}
VMEM = pl.BlockSpec(memory_space=pltpu.VMEM)
ANY = pl.BlockSpec(memory_space=pl.ANY)
GRANT = 12


def box_matrix(width):
    i = lax.broadcasted_iota(jnp.int32, (width, width), 0)
    j = lax.broadcasted_iota(jnp.int32, (width, width), 1)
    return jnp.where(jnp.abs(i - j) <= 4, 1.0, 0.0).astype(jnp.bfloat16)


def thirds(v):
    high = v.astype(jnp.bfloat16)
    rest = v - high.astype(jnp.float32)
    middle = rest.astype(jnp.bfloat16)
    low = (rest - middle.astype(jnp.float32)).astype(jnp.bfloat16)
    return high, middle, low


def depth_sums(read, planes):
    sums = []
    while len(sums) < planes:
        base = len(sums)
        if planes - base >= 8:
            back = [read(base + 7)]
            for k in range(6, -1, -1):
                back.append(back[-1] + read(base + k))
            ahead = read(base + 8)
            sums.append(back[7] + ahead)
            for k in range(1, 8):
                ahead = ahead + read(base + 8 + k)
                sums.append(back[7 - k] + ahead)
        else:
            p = [read(base + k) for k in range(12)]
            core = ((p[3] + p[4]) + (p[5] + p[6])) + (p[7] + p[8])
            a = p[1] + p[2]
            b = p[9] + p[10]
            sums += [core + (p[0] + a), core + (a + p[9]), core + (p[2] + b), core + (b + p[11])]
    return sums


def clear_rims(tz, rows):
    zero = jnp.zeros((8, tz.shape[-1]), jnp.float32)
    for w in range(tz.shape[0]):
        for i in range(tz.shape[1]):
            tz[w, i, 0:8, :] = zero
            tz[w, i, rows + 8 : rows + 16, :] = zero


def plane_sums(i, tz, t3, sx, box):
    windows, rows = tz.shape[0], tz.shape[2] - 16
    e = i % BLOCK
    for w in range(windows):
        for r in range(0, rows + 8, 8):
            t3[e, w, r : r + 8, :] = (
                tz[w, i, r + 3 : r + 11, :] + tz[w, i, r + 4 : r + 12, :] + tz[w, i, r + 5 : r + 13, :]
            )
    for group in GROUPS[windows]:
        parts = [
            thirds(t3[e, w, 1 : rows + 1, :] + t3[e, w, 4 : rows + 4, :] + t3[e, w, 7 : rows + 7, :]) for w in group
        ]
        sums = None
        for t in range(3):
            term = jnp.dot(
                jnp.concatenate([p[t] for p in parts], axis=0), box, preferred_element_type=jnp.float32
            )
            sums = term if sums is None else sums + term
        for k, w in enumerate(group):
            sx[w, e] = sums[rows * k : rows * (k + 1)]


def pair_weight(s_both, s_a, m_b, v_a, v_b):
    c = s_both - s_a * m_b
    return c, c / (v_a * v_b + EPSILON * CELLS * CELLS)


def row_blocks(rows, body):
    @pl.loop(0, rows // 16)
    def _(y):
        for half in range(2):
            r = pl.multiple_of(y * 16 + 8 * half, 8)
            body(pl.ds(r, 8), pl.ds(pl.multiple_of(r + 8, 8), 8))


def plane_of(parts, base):
    def read(a, p, rows):
        z = base + p
        for ref, offset, first, length in parts:
            if first <= z < first + length:
                return ref[a + offset, z - first, rows, :]
        raise ValueError("plane")

    return read


def own_block(read, stats, acc, z_out, tz, t3, sx, box):
    rows = tz.shape[2] - 16

    def body(here, there):
        zero = [read(0, p, here) for p in range(3 * BLOCK)]
        one = [read(1, p, here) for p in range(3 * BLOCK)]
        terms = [
            lambda p: zero[p],
            lambda p: zero[p] * zero[p],
            lambda p: one[p],
            lambda p: one[p] * one[p],
            lambda p: zero[p] * one[p],
        ]
        for w, term in enumerate(terms):
            for i, v in enumerate(depth_sums(term, BLOCK)):
                tz[w, i, there, :] = v

    row_blocks(rows, body)

    for i in range(BLOCK):
        plane_sums(i, tz, t3, sx, box)
        for y in range(0, rows, 8):
            r = slice(y, y + 8)
            s_0, q_0, s_1, q_1, both = [sx[w, i, r, :] for w in range(5)]
            m_0, m_1 = s_0 * (1.0 / CELLS), s_1 * (1.0 / CELLS)
            v_0 = q_0 - s_0 * m_0
            v_1 = q_1 - s_1 * m_1
            c, g = pair_weight(both, s_0, m_1, v_0, v_1)
            z = z_out + i
            stats[0, 0, z, r, :] = s_0
            stats[0, 1, z, r, :] = v_0
            stats[1, 0, z, r, :] = s_1
            stats[1, 1, z, r, :] = v_1
            acc[0, 0, z, r, :] = g * (read(1, BLOCK + i, r) - m_1)
            acc[1, 0, z, r, :] = g * (read(0, BLOCK + i, r) - m_0)
            gc = g * c
            acc[0, 1, z, r, :] = gc
            acc[1, 1, z, r, :] = gc


def own_inner_kernel(size, *refs):
    parts, (stats, acc, field, tz, t3, sx) = refs[: size + 2], refs[size + 2 :]
    rows, width = parts[0].shape[2:]
    clear_rims(tz, rows)
    box = box_matrix(width)
    for k, part in enumerate(parts):
        for a in range(2):
            field[a, BLOCK * k : BLOCK * (k + 1)] = part[a]

    @pl.loop(0, size)
    def _(j):
        own_block(lambda a, p, rows: field[a, BLOCK * j + p, rows, :], stats, acc, BLOCK * j, tz, t3, sx, box)


def own_ends_kernel(low, high, first, second, third, fourth, stats, acc, field, tz, t3, sx):
    rows, width = first.shape[2:]
    clear_rims(tz, rows)
    box = box_matrix(width)
    for e, parts in enumerate(((low, first, second), (third, fourth, high))):
        for k, part in enumerate(parts):
            for a in range(2):
                field[e, a, BLOCK * k : BLOCK * (k + 1)] = part[a]

    @pl.loop(0, 2)
    def _(e):
        own_block(lambda a, p, rows: field[e, a, p, rows, :], stats, acc, BLOCK * e, tz, t3, sx, box)


def side_group(planes, near, own, theirs, tables, tz, t3, sx, box, sink, done):
    rows = tz.shape[2] - 16
    far = 1 - near
    own_near, own_far = far, near

    def body(here, there):
        def n(p):
            return theirs(near, p, here)

        def f(p):
            return theirs(far, p, here)

        def square(read):
            def term(p):
                v = read(p)
                return v * v

            return term

        terms = [
            n,
            square(n),
            lambda p: n(p) * own(own_near, p, here),
            lambda p: n(p) * own(own_far, p, here),
            f,
            square(f),
            lambda p: f(p) * own(own_near, p, here),
        ]
        for w, term in enumerate(terms):
            for i, v in enumerate(depth_sums(term, planes)):
                tz[w, i, there, :] = v

    row_blocks(rows, body)

    for i in range(planes):
        plane_sums(i, tz, t3, sx, box)
        stats, z, acc, b = tables(i)
        for y in range(0, rows, 8):
            r = slice(y, y + 8)
            s_n, q_n, nn, fn, s_f, q_f, nf = [sx[w, i % BLOCK, r, :] for w in range(7)]
            o_s, o_v = stats[own_near, 0, z, r, :], stats[own_near, 1, z, r, :]
            p_s, p_v = stats[own_far, 0, z, r, :], stats[own_far, 1, z, r, :]
            m_n, m_f = s_n * (1.0 / CELLS), s_f * (1.0 / CELLS)
            v_n = q_n - s_n * m_n
            v_f = q_f - s_f * m_f
            off_n = theirs(near, BLOCK + i, r) - m_n
            off_f = theirs(far, BLOCK + i, r) - m_f
            c_nn, g_nn = pair_weight(nn, o_s, m_n, o_v, v_n)
            c_nf, g_nf = pair_weight(nf, o_s, m_f, o_v, v_f)
            c_fn, g_fn = pair_weight(fn, p_s, m_n, p_v, v_n)
            sink(own_near, i, r, acc[own_near, 0, b, r, :] + g_nn * off_n + g_nf * off_f,
                 acc[own_near, 1, b, r, :] + g_nn * c_nn + g_nf * c_nf, o_s, o_v)
            sink(own_far, i, r, acc[own_far, 0, b, r, :] + g_fn * off_n,
                 acc[own_far, 1, b, r, :] + g_fn * c_fn, p_s, p_v)
        done(i)


def readers(j, count, side, refs):
    depth = BLOCK * count
    own = [(ref, 0, BLOCK * k[1], BLOCK) for k, ref in refs.items() if k[0] == "own"]
    theirs = [(ref, 0, BLOCK * k[1], BLOCK) for k, ref in refs.items() if k[0] == "side"]
    for name, first in (("low", -BLOCK), ("high", depth)):
        if (name,) in refs:
            own.append((refs[name,], 0, first, BLOCK))
            theirs.append((refs[name,], 2 * side, first, BLOCK))
    base = BLOCK * (j - 1)
    return plane_of(own, base), plane_of(theirs, base)


def split_refs(keys, refs):
    return dict(zip(keys, refs[: len(keys)])), refs[len(keys) :]


def first_kernel(js, count, bases, keys, *refs):
    refs, (out, tz, t3, sx) = split_refs(keys, refs)
    near = lax.rem(lax.axis_index("phase"), 2)
    rows, width = refs["own", js[0]].shape[2:]
    clear_rims(tz, rows)
    own, theirs = readers(js[0], count, 1, refs)

    def tables(i):
        j, z = js[i // BLOCK], bases[i // BLOCK] + i % BLOCK
        return refs["stats", j], z, refs["acc", j], z

    def sink(a, i, r, one, two, s, v):
        out[a, 0, i, r, :] = one
        out[a, 1, i, r, :] = two

    side_group(BLOCK * len(js), near, own, theirs, tables, tz, t3, sx, box_matrix(width), sink, lambda i: None)


def last_kernel(js, count, bases, sums_base, before, final, keys, *refs):
    refs, rest = split_refs(keys, refs)
    if before is not None:
        out, rest = rest[0], rest[1:]
    if not final:
        block, rest = rest[0], rest[1:]
    tz, t3, sx, coef, padded, *rest = rest
    if final:
        block, rest = rest[0], rest[1:]
    planes = BLOCK * len(js)
    first = BLOCK * js[0]
    copies = []

    def write(source, first, sem):
        copy = pltpu.make_async_copy(source, out.at[:, :, first : first + source.shape[2]], sem)
        copy.start()
        copies.append(copy)

    if before is not None:
        sems = rest[0]
        write(refs["block",], BLOCK * before, sems.at[0])
    near = 1 - lax.rem(lax.axis_index("phase"), 2)
    rows, width = refs["own", js[0]].shape[2:]
    clear_rims(tz, rows)
    zero = jnp.zeros((8, width), jnp.float32)
    for a in range(2):
        padded[a, 0:8, :] = zero
        padded[a, rows + 8 : rows + 16, :] = zero
    lane = lax.broadcasted_iota(jnp.int32, (8, width), 1)
    own, theirs = readers(js[0], count, 2, refs)

    def tables(i):
        j = js[i // BLOCK]
        return refs["stats", j], bases[i // BLOCK] + i % BLOCK, refs["acc", j], sums_base[i // BLOCK] + i % BLOCK

    def sink(a, i, r, one, two, s, v):
        here = own(a, BLOCK + i, r) - s * (1.0 / CELLS)
        coef[a, i % BLOCK, r, :] = CELLS * (one - two / (v + EPSILON * CELLS) * here)

    def forces(i):
        for a in range(2):
            padded[a, 8 : rows + 8, :] = own(a, BLOCK + i, slice(0, rows))
            for y in range(0, rows, 8):
                r = slice(y, y + 8)
                c = coef[a, i % BLOCK, r, :]
                block[0, a, i, r, :] = c * (own(a, i + 5, r) - own(a, i + 3, r))
                block[1, a, i, r, :] = c * (padded[a, y + 9 : y + 17, :] - padded[a, y + 7 : y + 15, :])
                v = padded[a, y + 8 : y + 16, :]
                after_x = jnp.where(lane < width - 1, pltpu.roll(v, width - 1, 1), 0.0)
                before_x = jnp.where(lane > 0, pltpu.roll(v, 1, 1), 0.0)
                block[2, a, i, r, :] = c * (after_x - before_x)

    starts = [0] + [i for i in range(BLOCK, planes, BLOCK)] + [planes - 2, planes]

    def done(i):
        if i + 1 in starts:
            low = max(k for k in starts if k <= i)
            for k in range(low, i + 1):
                forces(k)
            if final:
                write(block.at[:, :, low : i + 1], first + low, sems.at[1 + starts.index(low)])

    side_group(planes, near, own, theirs, tables, tz, t3, sx, box_matrix(width), sink, done)
    for copy in copies:
        copy.wait()


def scratches(windows, rows, width, blocks=1):
    return [
        pltpu.VMEM((windows, BLOCK * blocks, rows + 16, width), jnp.float32),
        pltpu.VMEM((BLOCK, windows, rows + 8, width), jnp.float32),
        pltpu.VMEM((windows, BLOCK, rows, width), jnp.float32),
    ]


def params(mib=GRANT):
    return pltpu.CompilerParams(vmem_limit_bytes=mib << 20)


def like(*shape):
    return jax.ShapeDtypeStruct(shape, jnp.float32)


def cut_kernel(bs, images, *refs):
    outs, sems = refs[:-1], refs[-1]
    copies = [
        pltpu.make_async_copy(images.at[:, BLOCK * b : BLOCK * (b + 1)], outs[n], sems.at[n]) for n, b in enumerate(bs)
    ]
    for copy in copies:
        copy.start()
    for copy in copies:
        copy.wait()


def cut_blocks(bs, images, mib):
    phases, _, rows, width = images.shape
    outs = pl.pallas_call(
        functools.partial(cut_kernel, bs),
        out_shape=[like(phases, BLOCK, rows, width)] * len(bs),
        in_specs=[pl.BlockSpec(memory_space=pltpu.HBM)],
        out_specs=[VMEM] * len(bs),
        scratch_shapes=[pltpu.SemaphoreType.DMA((len(bs),))],
        compiler_params=params(mib),
    )(pltpu.with_memory_space_constraint(images, pltpu.HBM))
    return dict(zip(bs, outs))


def copied(source, target):
    for k in range(source.shape[0]):
        target[k] = source[k]


def pack_kernel(*refs):
    ends, tops, (inner, outer) = refs[:3], refs[3:6], refs[6:]
    even = lax.rem(lax.axis_index("slab"), 2) == 0

    def fill(target, parts):
        for k, part in enumerate(parts):
            for a in range(2):
                target[2 * k + a] = part[a]

    @pl.when(even)
    def _():
        fill(inner, ends)
        fill(outer, tops)

    @pl.when(jnp.logical_not(even))
    def _():
        fill(inner, tops)
        fill(outer, ends)


def unpack_kernel(inner, outer, low, high):
    even = lax.rem(lax.axis_index("slab"), 2) == 0

    @pl.when(even)
    def _():
        copied(outer, low)
        copied(inner, high)

    @pl.when(jnp.logical_not(even))
    def _():
        copied(inner, low)
        copied(outer, high)


def sorted_pair(kernel, operands, out):
    return pl.pallas_call(
        kernel, out_shape=(out, out), in_specs=[VMEM] * len(operands), out_specs=(VMEM, VMEM), compiler_params=params(6)
    )(*operands)


def swapped_rims(ends, tops):
    out = like(3 * ends[0].shape[0], *ends[0].shape[1:])
    n = lax.axis_size("slab")
    inner, outer = sorted_pair(pack_kernel, (*ends, *tops), out)
    pairs = [(q, q + 1) for q in range(1, n - 1, 2)] + [(q + 1, q) for q in range(1, n - 1, 2)]
    outer = lax.ppermute(outer, "slab", pairs)
    inner = lax.ppermute(inner, "slab", [(q, q ^ 1) for q in range(n)])
    return sorted_pair(unpack_kernel, (inner, outer), out)


def own_inner(low, high, blocks):
    rows, width = blocks[low].shape[2:]
    size = high - low
    shape = like(2, 2, BLOCK * size, rows, width)
    return pl.pallas_call(
        functools.partial(own_inner_kernel, size),
        out_shape=(shape, shape),
        in_specs=[VMEM] * (size + 2),
        out_specs=(VMEM, VMEM),
        scratch_shapes=[pltpu.VMEM((2, BLOCK * (size + 2), rows, width), jnp.float32)] + scratches(5, rows, width),
        compiler_params=params(),
    )(*[blocks[b] for b in range(low - 1, high + 1)])


def own_ends(low, high, *blocks):
    rows, width = low.shape[2:]
    shape = like(2, 2, 2 * BLOCK, rows, width)
    return pl.pallas_call(
        own_ends_kernel,
        out_shape=(shape, shape),
        in_specs=[VMEM] * 6,
        out_specs=(VMEM, VMEM),
        scratch_shapes=[pltpu.VMEM((2, 2, 3 * BLOCK, rows, width), jnp.float32)] + scratches(5, rows, width),
        compiler_params=params(),
        name="own_ends",
    )(low, high, *blocks)


def gather_operands(js, count, own, side, low, high):
    wanted = {}
    for b in range(js[0] - 1, js[-1] + 2):
        if 0 <= b < count:
            wanted["own", b] = own[b]
            wanted["side", b] = side[b]
        elif b < 0:
            wanted["low",] = low
        else:
            wanted["high",] = high
    return wanted


def specs_of(wanted):
    return [ANY if k == ("forces",) else VMEM for k in wanted]


def first_side(js, count, own, side, low, high, stats, accs, bases):
    rows, width = own[0].shape[2:]
    wanted = gather_operands(js, count, own, side, low, high)
    for j in js:
        wanted["stats", j], wanted["acc", j] = stats[j], accs[j]
    return pl.pallas_call(
        functools.partial(first_kernel, js, count, [bases[j] for j in js], tuple(wanted)),
        out_shape=like(2, 2, BLOCK * len(js), rows, width),
        in_specs=specs_of(wanted),
        out_specs=VMEM,
        scratch_shapes=scratches(7, rows, width, len(js)),
        compiler_params=params(),
    )(*wanted.values())


def last_side(js, count, own, side, low, high, stats, bases, sums, before, block, forces, final):
    rows, width = own[0].shape[2:]
    wanted = gather_operands(js, count, own, side, low, high)
    for j in js:
        wanted["stats", j], wanted["acc", j] = stats[j], sums[j][0]
    if before is not None:
        wanted["block",] = block
    if forces is not None:
        wanted["forces",] = forces
    whole = like(3, 2, BLOCK * count, rows, width)
    piece = (3, 2, BLOCK * len(js), rows, width)
    outs = ([(whole, ANY)] if before is not None else []) + ([] if final else [(like(*piece), VMEM)])
    got = pl.pallas_call(
        functools.partial(
            last_kernel, js, count, [bases[j] for j in js], [sums[j][1] for j in js], before, final, tuple(wanted)
        ),
        out_shape=[shape for shape, _ in outs],
        in_specs=specs_of(wanted),
        out_specs=[spec for _, spec in outs],
        input_output_aliases={len(wanted) - 1: 0} if forces is not None else {},
        scratch_shapes=scratches(7, rows, width, len(js))
        + [pltpu.VMEM((2, BLOCK, rows, width), jnp.float32), pltpu.VMEM((2, rows + 16, width), jnp.float32)]
        + ([pltpu.VMEM(piece, jnp.float32)] if final else [])
        + ([pltpu.SemaphoreType.DMA((2 + len(js) if final else 1,))] if before is not None else []),
        compiler_params=params(),
    )(*wanted.values())
    forces = got[0] if before is not None else None
    return forces, None if final else got[-1]


def across(value):
    n = lax.axis_size("phase")
    return lax.ppermute(value, "phase", [(q, q ^ 1) for q in range(n)])


def onward(value):
    n = lax.axis_size("phase")
    return lax.ppermute(value, "phase", [(q, (q + (2 if q % 2 == 0 else n - 2)) % n) for q in range(n)])


def yonder(value):
    n = lax.axis_size("phase")
    return lax.ppermute(value, "phase", [(q, (q + (n - 2 if q % 2 == 0 else 2)) % n) for q in range(n)])


def local_forces(images):
    count = images.shape[1] // BLOCK
    assert images.shape[0] == 2 and images.shape[1] == BLOCK * count and count >= 6
    assert lax.axis_size("phase") % 2 == 0 and lax.axis_size("slab") % 2 == 0
    half = (count + 1) // 2

    top, end, turned = 0, count - 1, count - 2
    blocks = cut_blocks((top,), images, 4)
    blocks.update(cut_blocks((end, turned), images, 4))
    blocks.update(cut_blocks(tuple(range(1, turned)), images, 4))
    one = {b: across(blocks[b]) for b in blocks}
    two = {b: onward(one[b]) for b in blocks if b != turned}
    two[turned] = across(yonder(blocks[turned]))
    low, high = swapped_rims((blocks[end], one[end], two[end]), (blocks[top], one[top], two[top]))

    near_half = own_inner(1, half, blocks)
    far_half = own_inner(half, count - 1, blocks)
    outer = own_ends(low, high, blocks[0], blocks[1], blocks[end - 1], blocks[end])
    stats, acc, base = {}, {}, {}
    for j in range(count):
        if j in (0, count - 1):
            (stats[j], acc[j]), base[j] = outer, 0 if j == 0 else BLOCK
        elif j < half:
            (stats[j], acc[j]), base[j] = near_half, BLOCK * (j - 1)
        else:
            (stats[j], acc[j]), base[j] = far_half, BLOCK * (j - half)
    sums = {}
    for js in first_groups(count):
        total = first_side(js, count, blocks, one, low, high, stats, acc, base)
        sums.update({j: (total, BLOCK * k) for k, j in enumerate(js)})
    forces, block, before = None, None, None
    groups = last_groups(count)
    for js in groups:
        forces, block = last_side(
            js, count, blocks, two, low, high, stats, base, sums, before, block, forces, js == groups[-1]
        )
        before = js[0]
    return forces


def first_groups(count):
    return [(j,) for j in range(count - 3)] + [tuple(range(count - 3, count))]


def last_groups(count):
    return [(j,) for j in (1, 2, 0, *range(3, count - 3))] + [tuple(range(count - 3, count))]


def solution(mesh):
    in_specs = (P("phase", "slab", None, None),)
    out_specs = P(None, "phase", "slab", None, None)
    return jax.shard_map(local_forces, mesh=mesh, in_specs=in_specs, out_specs=out_specs, check_vma=False)
```
